128 devices in a mesh: dom: 128 (over x, z, y, core).
Axes of the slice: x: 4, y: 4, z: 4, core: 2. Of those that a mesh axis runs over, the one named last changes fastest.
Arguments:
- adjoint_end: bfloat16 [1024, 384, 256], P('dom'), may hold values from -6 to 6
- operator_blocks: bfloat16 [1024, 6, 384, 384], P('dom'), may hold values from -0.125 to 0.125
- block_cols: int32 [1024, 6], P('dom'), may hold values from -1 to 15, as said below
- halo_send: int32 [128, 4, 2], P('dom'), may hold values from -1 to 7, as said below
- wet_cells: int32 [1024, 128], P('dom'), may hold values 0 or 1
- gauge_cells: int32 [256], replicated, may hold values from 0 to 131071
- window_first: int32 [256], replicated, may hold values from 0 to 1
- window_len: int32 [256], replicated, may hold values from 1 to 2
- gauge_gain: float32 [256], replicated, may hold values from 0.5 to 4
- snapshots: float32 [2, 1024, 384], P(None, 'dom'), may hold values from -27 to 27, as said below
Outputs:
- adjoint_start: bfloat16 [1024, 384, 256], P('dom')
- sensitivity: float32 [1024, 128, 256], P('dom')
The draws below stay inside these ranges and needn't reach their ends.
Inputs may be any that keep to these rules, and one draw needn't show every extreme that they name: `block_cols`: in each row entry 0 is the row's own local block; live entries come first and -1 fills the rest; received slots named are only those whose sending device exists. `halo_send`: for each device and neighbour o the 2 blocks are distinct; -1 exactly where device d + off_o does not exist. `snapshots`: nonzero values.
All inputs are finite; a program needn't handle non-finite values. No bound on the sum of `wet_cells` on one device may be relied on, other than what follows from the above.
Results may differ from the reference program's by a relative error of at most 0.0013.
The reference program's roundings to bfloat16 on the way count: a program that leaves them out, or rounds other values in their place, can miss the bound.
Values may be sent and summed in bfloat16 or wider, within the bound.
A program may use at most 128 MiB of HBM per device.

```python
import math
import jax
import jax.numpy as jnp
from jax import lax

BD = 8
CB = 128
NF = 256
KN = 6
CAP = 2
STEPS = 2
BLOCKS = 1024
CELLS = 131072


neighbour_offsets = (-2, -1, 1, 2)


def topology(key):
    devices = BLOCKS // BD
    offsets = jnp.array(neighbour_offsets, jnp.int32)
    key_pick, key_heavy, key_own = jax.random.split(jax.random.fold_in(key, 7), 3)
    pick_keys = jax.random.split(key_pick, devices * 4)
    picks = jax.vmap(lambda single: jax.random.permutation(single, BD)[:CAP])(pick_keys).reshape(devices, 4, CAP)
    device_ids = jnp.arange(devices, dtype=jnp.int32)[:, None]
    target = device_ids + offsets[None, :]
    exists = (target >= 0) & (target < devices)
    sends = jnp.where(exists[:, :, None], picks, -1).astype(jnp.int32)
    source = device_ids - offsets[None, :]
    arrives = (source >= 0) & (source < devices)
    heavy = jax.random.randint(key_heavy, (devices,), 0, 4) == 0
    heavy = heavy.at[0].set(False).at[1].set(True)
    lighter = min(KN, 1 + (4 * CAP + BD - 1) // BD)
    live = jnp.where(heavy, KN, lighter).astype(jnp.int32)[:, None, None]
    row_ids = jnp.arange(BD, dtype=jnp.int32)[None, :, None]
    entry = jnp.arange(KN, dtype=jnp.int32)[None, None, :]
    position = row_ids * (live - 1) + entry - 1
    slot_group = jnp.clip(position // CAP, 0, 3)
    group_ids = jnp.arange(4, dtype=jnp.int32)
    arrived = jnp.any((slot_group[:, :, :, None] == group_ids) & arrives[:, None, None, :], axis=-1)
    use_halo = (entry >= 1) & (position >= 0) & (position < 4 * CAP) & arrived
    own_pick = jax.random.randint(key_own, (devices, BD, KN), 0, BD)
    columns = jnp.where(entry == 0, row_ids, jnp.where(use_halo, BD + position, own_pick))
    columns = jnp.where(entry < live, columns, -1).astype(jnp.int32)
    return (columns.reshape(devices * BD, KN), sends)


def draw_block_cols(key, part):
    return topology(key)[0]


def draw_halo_send(key, part):
    return topology(key)[1]


def draw_snapshots(key, part):
    key_mag, key_sign = jax.random.split(jax.random.fold_in(key, 11), 2)
    shape = (STEPS, BLOCKS, 3 * CB)
    along = jnp.arange(BLOCKS, dtype=jnp.float32)[None, :, None] / (BLOCKS - 1)
    signs = jnp.where(jax.random.bernoulli(key_sign, 0.5, shape), 1.0, -1.0)
    rise = 1.0 + 2.0 * along
    magnitude = jnp.exp(jax.random.uniform(key_mag, shape, jnp.float32, jnp.log(0.3), jnp.log(3.0)))
    return (signs * magnitude * rise).astype(jnp.float32)


def set_ends(values, stream_key, least, top_value):
    index_at = [jax.random.randint(jax.random.fold_in(stream_key, axis), (), 0, length) for axis, length in enumerate(values.shape)]
    longest = values.shape.index(max(values.shape))
    beside = index_at[:longest] + [(index_at[longest] + 1) % values.shape[longest]] + index_at[longest + 1:]
    return values.at[tuple(index_at)].set(least).at[tuple(beside)].set(top_value)


def block_levels(own_key, shape, shards, smallest, top_value):
    def one(axis_at, parts):
        draws = jax.random.uniform(jax.random.fold_in(jax.random.fold_in(own_key, 6), axis_at), (parts,), jnp.float32, smallest / len(shards), top_value / len(shards))
        return jnp.repeat(jnp.exp(draws), shape[axis_at] // parts).reshape((-1,) + (1,) * (len(shape) - axis_at - 1))

    level = one(*shards[0])
    for cut in shards[1:]:
        level = level * one(*cut)
    return level


def noise(own_key, dims, scale, most, cuts=(), kind=jnp.bfloat16):
    gain = block_levels(own_key, dims, cuts, -0.22, 0.18) if cuts else 1.0
    drawn = jax.random.normal(own_key, dims, jnp.float32) * scale * gain
    return jnp.minimum(jnp.maximum(drawn, -most), most).astype(kind)


def setup_inputs(seed: int = 0) -> dict:
    splits = jax.random.split(jax.random.key(seed), 11)
    adjoint_end = noise(splits[0], (BLOCKS, 3 * CB, NF), 1.0, 6.0, ((0, 128),))
    operator_blocks = noise(splits[1], (BLOCKS, KN, 3 * CB, 3 * CB), (3 * CB * KN) ** -0.5, 0.125, ((0, 128),))
    block_cols = draw_block_cols(jax.random.fold_in(splits[10], 71), 0)
    halo_send = draw_halo_send(jax.random.fold_in(splits[10], 71), 0)
    wet_cells = set_ends((jax.random.randint(splits[4], (BLOCKS, CB), 0, 4) < 3).astype(jnp.int32), jax.random.fold_in(splits[4], 1), 0, 1)
    gauge_cells = set_ends(jax.random.randint(splits[5], (NF,), 0, CELLS), jax.random.fold_in(splits[5], 1), 0, CELLS - 1).astype(jnp.int32)
    window_first = set_ends(jax.random.randint(splits[6], (NF,), 0, STEPS), jax.random.fold_in(splits[6], 1), 0, STEPS - 1).astype(jnp.int32)
    window_len = set_ends(jax.random.randint(splits[7], (NF,), 1, STEPS + 1), jax.random.fold_in(splits[7], 1), 1, STEPS).astype(jnp.int32)
    gauge_gain = jnp.clip(jnp.exp(jax.random.uniform(splits[8], (NF,), jnp.float32, math.log(0.5), math.log(4.0))), 0.5, 4.0)
    snapshots = draw_snapshots(jax.random.fold_in(splits[10], 71), 0)
    return {"adjoint_end": adjoint_end, "operator_blocks": operator_blocks, "block_cols": block_cols, "halo_send": halo_send, "wet_cells": wet_cells, "gauge_cells": gauge_cells, "window_first": window_first, "window_len": window_len, "gauge_gain": gauge_gain, "snapshots": snapshots}


neighbour_offsets = (-2, -1, 1, 2)

def global_columns(block_cols, halo_send):
    devices = BLOCKS // BD
    offsets = jnp.array(neighbour_offsets, jnp.int32)
    row_device = (jnp.arange(BLOCKS, dtype=jnp.int32) // BD)[:, None]
    own_block = row_device * BD + jnp.clip(block_cols, 0, BD - 1)
    slot_number = jnp.clip(block_cols - BD, 0, 4 * CAP - 1)
    group = slot_number // CAP
    within = slot_number % CAP
    sender = jnp.clip(row_device - offsets[group], 0, devices - 1)
    sent_block = halo_send[sender, group, within]
    remote_block = sender * BD + jnp.clip(sent_block, 0, BD - 1)
    glob = jnp.where(block_cols < BD, own_block, remote_block).astype(jnp.int32)
    return (glob, block_cols >= 0)

def reference(adjoint_end, operator_blocks, block_cols, halo_send, wet_cells, gauge_cells, window_first, window_len, gauge_gain, snapshots):
    glob, valid = global_columns(block_cols, halo_send)
    cell_ids = jnp.arange(CELLS, dtype=jnp.int32).reshape(BLOCKS, CB)
    gauge_hit = (cell_ids[:, :, None] == gauge_cells[None, None, :]).astype(jnp.float32)
    wet_rows = jnp.tile(wet_cells.astype(jnp.float32), (1, 3))[:, :, None]
    adjoint = adjoint_end
    raw = jnp.zeros((BLOCKS, CB, NF), jnp.float32)
    for step_index in range(STEPS):
        current = adjoint

        def one_row(items):
            columns, usable, weights = items
            picked = current[columns].astype(jnp.float32)
            picked = jnp.where(usable[:, None, None], picked, jnp.zeros((), jnp.float32))
            return jnp.einsum('kij,kjf->if', weights.astype(jnp.float32), picked)
        coupled = lax.map(one_row, (glob, valid, operator_blocks))
        active = ((window_first <= step_index) & (step_index < window_first + window_len)).astype(jnp.float32) * gauge_gain
        source = gauge_hit * active[None, None, :]
        source_full = jnp.concatenate([source, jnp.zeros((BLOCKS, 2 * CB, NF), jnp.float32)], axis=1)
        updated = wet_rows * (current.astype(jnp.float32) + coupled) + source_full
        adjoint = updated.astype(jnp.bfloat16)
        saved = snapshots[step_index].reshape(BLOCKS, 3, CB)[:, :, :, None]
        raw = raw + lax.optimization_barrier(jnp.sum(saved * adjoint.astype(jnp.float32).reshape(BLOCKS, 3, CB, NF), axis=1))
    meansq = lax.optimization_barrier(jnp.sum(raw * raw, axis=(0, 1))) / CELLS
    sensitivity = raw * lax.rsqrt(meansq + 1e-06)[None, None, :]
    return (adjoint, sensitivity)
```

```python
import functools

import jax
import jax.numpy as jnp
from jax import lax
from jax.experimental import pallas as pl
from jax.experimental.pallas import tpu as pltpu
from jax.sharding import PartitionSpec as P

neighbour_offsets = (-2, -1, 1, 2)
MESH = pl.DeviceIdType.MESH
LANES = 128
STEPS = 2


def kernel(
    devices,
    line,
    adj_hbm,
    ops_hbm,
    cols_hbm,
    lists_hbm,
    wet_hbm,
    cells_hbm,
    first_hbm,
    length_hbm,
    gain_hbm,
    snap_hbm,
    adj_out,
    sens_out,
    *scratch,
):
    names = iter(scratch)
    take = lambda n: [next(names) for _ in range(n)]
    (ops,) = take(1)
    ext = [take(2), take(2)]
    own = [take(2), take(2)]
    sent = [take(2), take(2)]
    final = take(2)
    raw = take(2)
    sens = take(2)
    snap_b, wet_b = take(2)
    columns_m, cols, lists = take(3)
    functional = take(4)
    mine = take(2)
    line_sum = take(2)
    from_line = take(2)
    from_plane = take(2)
    in_sem, ops_sem, send_sem, recv_sem, line_send, line_recv, plane_send, plane_recv, out_sem = take(9)

    owned, rows = own[0][0].shape[0], own[0][0].shape[1]
    entries = ops.shape[1]
    cells = rows // 3
    capacity = 2
    me = lax.axis_index("dom")
    planes = devices // line

    loads = []

    def load(src, dst):
        copy = pltpu.make_async_copy(src, dst, in_sem.at[len(loads)])
        copy.start()
        loads.append(copy)
        return copy

    lists_in = load(lists_hbm, lists)
    adj_in = []
    for h in range(2):
        half = adj_hbm.at[:, :, pl.ds(h * LANES, LANES)]
        adj_in.append(load(half, own[0][h]))
    ext_in = []
    for h in range(2):
        half = adj_hbm.at[:, :, pl.ds(h * LANES, LANES)]
        ext_in.append(load(half, ext[0][h].at[pl.ds(0, owned)]))
    small_in = [load(cols_hbm, cols)]
    for s in range(STEPS):
        for c in range(3):
            small_in.append(
                load(
                    snap_hbm.at[s, :, pl.ds(c * cells, cells)],
                    columns_m.at[pl.ds((s * 3 + c) * owned, owned)],
                )
            )
    for src, dst in zip((cells_hbm, first_hbm, length_hbm, gain_hbm), functional[:4]):
        small_in.append(load(src, dst))
    wet_i = next(names)
    small_in.append(load(wet_hbm, wet_i))
    ops_in = []
    for b in range(owned):
        copy = pltpu.make_async_copy(ops_hbm.at[b], ops.at[b], ops_sem.at[b])
        copy.start()
        ops_in.append(copy)

    barrier = pltpu.get_barrier_semaphore()
    greeted = jnp.int32(line - 1 + planes - 1)
    exists = []
    for offset in neighbour_offsets:
        target = me + offset
        there = (target >= 0) & (target < devices)
        exists.append(there)
        greeted = greeted + there.astype(jnp.int32)

        @pl.when(there)
        def _():
            pl.semaphore_signal(barrier, inc=1, device_id=(target,), device_id_type=MESH)

    def line_peer(j):
        return (me // line) * line + lax.rem(me + j, line)

    def plane_peer(j):
        return lax.rem(me + j * line, devices)

    for j in range(1, line):
        pl.semaphore_signal(barrier, inc=1, device_id=(line_peer(j),), device_id_type=MESH)
    for j in range(1, planes):
        pl.semaphore_signal(barrier, inc=1, device_id=(plane_peer(j),), device_id_type=MESH)

    for s in range(STEPS):
        for h in range(2):
            ext[s][h][2 * owned] = jnp.zeros((rows, LANES), jnp.bfloat16)

    def halo_copy(s, h, group):
        return pltpu.make_async_remote_copy(
            src_ref=sent[s][h].at[pl.ds(group * capacity, capacity)],
            dst_ref=ext[s][h].at[pl.ds(owned + group * capacity, capacity)],
            send_sem=send_sem.at[s, h, group],
            recv_sem=recv_sem.at[s, h, group],
            device_id=(jnp.clip(me + neighbour_offsets[group], 0, devices - 1),),
            device_id_type=MESH,
        )

    def gather(s, h):
        for group in range(4):
            for c in range(capacity):
                block = jnp.maximum(lists[0, group, c], 0)
                sent[s][h][group * capacity + c] = own[s][h][block]

    def send(s, h):
        for group in (0, 3, 1, 2):

            @pl.when(exists[group])
            def _():
                halo_copy(s, h, group).start()

    def await_halo(s, h):
        for group in range(4):

            @pl.when(exists[3 - group])
            def _():
                halo_copy(s, h, group).wait_recv()

    lists_in.wait()
    adj_in[0].wait()
    gather(0, 0)
    pl.semaphore_wait(barrier, greeted)
    send(0, 0)
    adj_in[1].wait()
    gather(0, 1)
    send(0, 1)

    for copy in small_in:
        copy.wait()
    used = 2 * 3 * owned
    columns_m[pl.ds(used, owned)] = wet_i[...].astype(jnp.float32)
    turned = jnp.transpose(columns_m[...])
    for s in range(STEPS):
        for c in range(3):
            for b in range(owned):
                at = (s * 3 + c) * owned + b
                snap_b[s, b, pl.ds(c * cells, cells)] = jnp.broadcast_to(
                    turned[:, at : at + 1], (cells, LANES)
                )
    for b in range(owned):
        at = used + b
        wet_b[b] = jnp.broadcast_to(turned[:, at : at + 1], (cells, LANES))

    for copy in ext_in:
        copy.wait()
    for copy in ops_in:
        copy.wait()

    row_in_block = lax.broadcasted_iota(jnp.int32, (cells, LANES), 0)

    def advance(s, h):
        part = pl.ds(h * LANES, LANES)
        at_cell = functional[0][:, part]
        first = functional[1][:, part]
        active = jnp.where(
            (first <= s) & (s < first + functional[2][:, part]), functional[3][:, part], 0.0
        )

        def one_row(b, squares):
            picked = []
            for k in range(entries):
                col = cols[b, k]
                picked.append(ext[s][h][jnp.where(col < 0, 2 * owned, col)])
            coupled = jnp.dot(
                jnp.concatenate([ops[b, k] for k in range(entries)], axis=1),
                jnp.concatenate(picked, axis=0),
                preferred_element_type=jnp.float32,
            )
            wet = wet_b[b]
            here = row_in_block + (me * owned + b) * cells
            source = jnp.where(here == at_cell, active, 0.0)
            total = None
            for c in range(3):
                piece = slice(c * cells, (c + 1) * cells)
                now = own[s][h][b, piece].astype(jnp.float32)
                updated = wet * (now + coupled[piece])
                if c == 0:
                    updated = updated + source
                rounded = updated.astype(jnp.bfloat16)
                if s + 1 < STEPS:
                    own[s + 1][h][b, piece] = rounded
                    ext[s + 1][h][b, piece] = rounded
                else:
                    final[h][b, piece] = rounded
                term = snap_b[s, b, piece] * rounded.astype(jnp.float32)
                total = term if total is None else total + term
            if s > 0:
                total = raw[h][b] + total
            raw[h][b] = total
            if s + 1 < STEPS:
                return squares
            return squares + jnp.sum((total * total).reshape(cells // 8, 8, LANES), axis=0)

        return lax.fori_loop(0, owned, one_row, jnp.zeros((8, LANES), jnp.float32))

    def line_copy(h, j):
        return pltpu.make_async_remote_copy(
            src_ref=mine[h],
            dst_ref=from_line[h].at[j - 1],
            send_sem=line_send.at[h, j - 1],
            recv_sem=line_recv.at[h, j - 1],
            device_id=(line_peer(j),),
            device_id_type=MESH,
        )

    def plane_copy(h, j):
        return pltpu.make_async_remote_copy(
            src_ref=line_sum[h],
            dst_ref=from_plane[h].at[j - 1],
            send_sem=plane_send.at[h, j - 1],
            recv_sem=plane_recv.at[h, j - 1],
            device_id=(plane_peer(j),),
            device_id_type=MESH,
        )

    def reduce_line_start(h, squares):
        mine[h][...] = jnp.sum(squares, axis=0, keepdims=True)
        for j in range(1, line):
            line_copy(h, j).start()

    def reduce_plane_start(h):
        total = mine[h][...]
        for j in range(1, line):
            line_copy(h, j).wait_recv()
            total = total + from_line[h][j - 1]
        line_sum[h][...] = total
        for j in range(1, planes):
            plane_copy(h, j).start()

    def finish(h):
        total = line_sum[h][...]
        for j in range(1, planes):
            plane_copy(h, j).wait_recv()
            total = total + from_plane[h][j - 1]
        meansq = total / (devices * owned * cells)
        scale = lax.rsqrt(meansq + 1e-6)
        for b in range(owned):
            sens[h][b] = raw[h][b] * scale
        copy = pltpu.make_async_copy(
            sens[h], sens_out.at[:, :, pl.ds(h * LANES, LANES)], out_sem.at[1, h]
        )
        copy.start()
        return copy

    def put_final(h):
        copy = pltpu.make_async_copy(
            final[h], adj_out.at[:, :, pl.ds(h * LANES, LANES)], out_sem.at[0, h]
        )
        copy.start()
        return copy

    for h in range(2):
        await_halo(0, h)
        advance(0, h)
        gather(1, h)
        send(1, h)

    puts = []
    await_halo(1, 0)
    squares = advance(1, 0)
    reduce_line_start(0, squares)
    puts.append(put_final(0))
    await_halo(1, 1)
    reduce_plane_start(0)
    squares = advance(1, 1)
    reduce_line_start(1, squares)
    puts.append(put_final(1))
    puts.append(finish(0))
    reduce_plane_start(1)
    puts.append(finish(1))

    for s in range(STEPS):
        for h in range(2):
            for group in range(4):

                @pl.when(exists[group])
                def _():
                    halo_copy(s, h, group).wait_send()

    for h in range(2):
        for j in range(1, line):
            line_copy(h, j).wait_send()
        for j in range(1, planes):
            plane_copy(h, j).wait_send()
    for copy in puts:
        copy.wait()


def per_device(
    adjoint_end,
    operator_blocks,
    block_cols,
    halo_send,
    wet_cells,
    gauge_cells,
    window_first,
    window_len,
    gauge_gain,
    snapshots,
):
    devices = lax.axis_size("dom")
    owned, rows, width = adjoint_end.shape
    entries = operator_blocks.shape[1]
    cells = rows // 3
    line = 8
    bf16, f32, i32 = jnp.bfloat16, jnp.float32, jnp.int32
    slots = 2 * owned + 1
    scratch = (
        [pltpu.VMEM((owned, entries, rows, rows), bf16)]
        + [pltpu.VMEM((slots, rows, LANES), bf16)] * 4
        + [pltpu.VMEM((owned, rows, LANES), bf16)] * 4
        + [pltpu.VMEM((owned, rows, LANES), bf16)] * 4
        + [pltpu.VMEM((owned, rows, LANES), bf16)] * 2
        + [pltpu.VMEM((owned, cells, LANES), f32)] * 2
        + [pltpu.VMEM((owned, cells, LANES), f32)] * 2
        + [
            pltpu.VMEM((STEPS, owned, rows, LANES), f32),
            pltpu.VMEM((owned, cells, LANES), f32),
            pltpu.VMEM((LANES, LANES), f32),
            pltpu.SMEM(block_cols.shape, i32),
            pltpu.SMEM(halo_send.shape, i32),
        ]
        + [pltpu.VMEM((1, width), i32)] * 3
        + [pltpu.VMEM((1, width), f32)]
        + [pltpu.VMEM((1, LANES), f32)] * 4
        + [pltpu.VMEM((line - 1, 1, LANES), f32)] * 2
        + [pltpu.VMEM((devices // line - 1, 1, LANES), f32)] * 2
        + [
            pltpu.SemaphoreType.DMA((17,)),
            pltpu.SemaphoreType.DMA((owned,)),
            pltpu.SemaphoreType.DMA((STEPS, 2, 4)),
            pltpu.SemaphoreType.DMA((STEPS, 2, 4)),
            pltpu.SemaphoreType.DMA((2, line - 1)),
            pltpu.SemaphoreType.DMA((2, line - 1)),
            pltpu.SemaphoreType.DMA((2, devices // line - 1)),
            pltpu.SemaphoreType.DMA((2, devices // line - 1)),
            pltpu.SemaphoreType.DMA((2, 2)),
            pltpu.VMEM(wet_cells.shape, i32),
        ]
    )
    anywhere = pl.BlockSpec(memory_space=pl.ANY)
    row = lambda v: v.reshape(1, width)
    return pl.pallas_call(
        functools.partial(kernel, devices, line),
        out_shape=(
            jax.ShapeDtypeStruct(adjoint_end.shape, bf16),
            jax.ShapeDtypeStruct((owned, cells, width), f32),
        ),
        in_specs=[anywhere] * 10,
        out_specs=(anywhere, anywhere),
        scratch_shapes=scratch,
        compiler_params=pltpu.CompilerParams(
            collective_id=0, has_side_effects=True, vmem_limit_bytes=56 * 1024 * 1024
        ),
        name="adjoint",
    )(
        adjoint_end,
        operator_blocks,
        block_cols,
        halo_send,
        wet_cells,
        row(gauge_cells),
        row(window_first),
        row(window_len),
        row(gauge_gain),
        snapshots,
    )


def solution(mesh):
    return jax.shard_map(
        per_device,
        mesh=mesh,
        in_specs=(
            P("dom", None, None),
            P("dom", None, None, None),
            P("dom", None),
            P("dom", None, None),
            P("dom", None),
            P(),
            P(),
            P(),
            P(),
            P(None, "dom", None),
        ),
        out_specs=(P("dom", None, None), P("dom", None, None)),
        check_vma=False,
    )
```

```python
import functools

import jax
import jax.numpy as jnp
from jax import lax
from jax.experimental import pallas as pl
from jax.experimental.pallas import tpu as pltpu
from jax.sharding import PartitionSpec as P

neighbour_offsets = (-2, -1, 1, 2)
MESH = pl.DeviceIdType.MESH
LANES = 128
STEPS = 2
UNROLL = 4
VM = 44


def kernel(
    devices,
    line,
    adj_hbm,
    ops_hbm,
    cols_hbm,
    lists_hbm,
    wet_hbm,
    cells_hbm,
    first_hbm,
    length_hbm,
    gain_hbm,
    snap_hbm,
    adj_out,
    sens_out,
    *scratch,
):
    names = iter(scratch)
    take = lambda n: [next(names) for _ in range(n)]
    (ops,) = take(1)
    ext = [take(2), take(2)]
    own = [take(2), take(2)]
    sent = [take(2), take(2)]
    final = take(2)
    raw = take(2)
    sens = take(2)
    snap_b, wet_b = take(2)
    columns_m, cols, lists = take(3)
    functional = take(4)
    mine = take(2)
    line_sum = take(2)
    from_line = take(2)
    from_plane = take(2)
    in_sem, ops_sem, send_sem, recv_sem, line_send, line_recv, plane_send, plane_recv, out_sem = take(9)

    owned, rows = own[0][0].shape[0], own[0][0].shape[1]
    entries = ops.shape[1]
    cells = rows // 3
    capacity = 2
    me = lax.axis_index("dom")
    planes = devices // line

    loads = []

    def load(src, dst):
        copy = pltpu.make_async_copy(src, dst, in_sem.at[len(loads)])
        copy.start()
        loads.append(copy)
        return copy

    lists_in = load(lists_hbm, lists)
    adj_in = []
    for h in range(2):
        half = adj_hbm.at[:, :, pl.ds(h * LANES, LANES)]
        adj_in.append(load(half, own[0][h]))
    ext_in = []
    for h in range(2):
        half = adj_hbm.at[:, :, pl.ds(h * LANES, LANES)]
        ext_in.append(load(half, ext[0][h].at[pl.ds(0, owned)]))
    small_in = [load(cols_hbm, cols)]
    for s in range(STEPS):
        for c in range(3):
            small_in.append(
                load(
                    snap_hbm.at[s, :, pl.ds(c * cells, cells)],
                    columns_m.at[pl.ds((s * 3 + c) * owned, owned)],
                )
            )
    for src, dst in zip((cells_hbm, first_hbm, length_hbm, gain_hbm), functional[:4]):
        small_in.append(load(src, dst))
    wet_i = next(names)
    small_in.append(load(wet_hbm, wet_i))
    ops_in = []
    for b in range(owned):
        copy = pltpu.make_async_copy(ops_hbm.at[b], ops.at[b], ops_sem.at[b])
        copy.start()
        ops_in.append(copy)

    barrier = pltpu.get_barrier_semaphore()
    greeted = jnp.int32(line - 1 + planes - 1)
    exists = []
    for offset in neighbour_offsets:
        target = me + offset
        there = (target >= 0) & (target < devices)
        exists.append(there)
        greeted = greeted + there.astype(jnp.int32)

        @pl.when(there)
        def _():
            pl.semaphore_signal(barrier, inc=1, device_id=(target,), device_id_type=MESH)

    def line_peer(j):
        return (me // line) * line + lax.rem(me + j, line)

    def plane_peer(j):
        return lax.rem(me + j * line, devices)

    for j in range(1, line):
        pl.semaphore_signal(barrier, inc=1, device_id=(line_peer(j),), device_id_type=MESH)
    for j in range(1, planes):
        pl.semaphore_signal(barrier, inc=1, device_id=(plane_peer(j),), device_id_type=MESH)

    for s in range(STEPS):
        for h in range(2):
            ext[s][h][2 * owned] = jnp.zeros((rows, LANES), jnp.bfloat16)

    def halo_copy(s, h, group):
        return pltpu.make_async_remote_copy(
            src_ref=sent[s][h].at[pl.ds(group * capacity, capacity)],
            dst_ref=ext[s][h].at[pl.ds(owned + group * capacity, capacity)],
            send_sem=send_sem.at[s, h, group],
            recv_sem=recv_sem.at[s, h, group],
            device_id=(jnp.clip(me + neighbour_offsets[group], 0, devices - 1),),
            device_id_type=MESH,
        )

    def gather(s, h):
        for group in range(4):
            for c in range(capacity):
                block = jnp.maximum(lists[0, c, group], 0)
                sent[s][h][group * capacity + c] = own[s][h][block]

    odd = lax.rem(me, 2)
    light = (odd == 1, False, False, odd == 0)

    def send(s, h, which=None):
        for group in (0, 3, 1, 2):
            go = exists[group]
            if which is not None:
                held = jnp.logical_and(light[group], go)
                go = held if which == "held" else jnp.logical_and(jnp.logical_not(light[group]), go)

            @pl.when(go)
            def _():
                halo_copy(s, h, group).start()

    def await_halo(s, h):
        for group in range(4):

            @pl.when(exists[3 - group])
            def _():
                halo_copy(s, h, group).wait_recv()

    lists_in.wait()
    adj_in[0].wait()
    gather(0, 0)
    pl.semaphore_wait(barrier, greeted)
    send(0, 0)
    adj_in[1].wait()
    gather(0, 1)
    send(0, 1, "first")

    for copy in small_in:
        copy.wait()
    used = 2 * 3 * owned
    columns_m[pl.ds(used, owned)] = wet_i[...].astype(jnp.float32)
    turned = jnp.transpose(columns_m[...])
    for s in range(STEPS):
        for c in range(3):
            for b in range(owned):
                at = (s * 3 + c) * owned + b
                snap_b[s, b, pl.ds(c * cells, cells)] = jnp.broadcast_to(
                    turned[:, at : at + 1], (cells, LANES)
                )
    for b in range(owned):
        at = used + b
        wet_b[b] = jnp.broadcast_to(turned[:, at : at + 1], (cells, LANES))

    for copy in ext_in:
        copy.wait()
    for copy in ops_in:
        copy.wait()

    row_in_block = lax.broadcasted_iota(jnp.int32, (cells, LANES), 0)

    def advance(s, h):
        part = pl.ds(h * LANES, LANES)
        at_cell = functional[0][:, part]
        first = functional[1][:, part]
        active = jnp.where(
            (first <= s) & (s < first + functional[2][:, part]), functional[3][:, part], 0.0
        )

        def one_row(b, squares):
            picked = []
            for k in range(entries):
                col = cols[b, k]
                picked.append(ext[s][h][jnp.where(col < 0, 2 * owned, col)])
            coupled = jnp.dot(
                jnp.concatenate([ops[b, k] for k in range(entries)], axis=1),
                jnp.concatenate(picked, axis=0),
                preferred_element_type=jnp.float32,
            )
            wet = wet_b[b]
            here = row_in_block + (me * owned + b) * cells
            source = jnp.where(here == at_cell, active, 0.0)
            total = None
            for c in range(3):
                piece = slice(c * cells, (c + 1) * cells)
                now = own[s][h][b, piece].astype(jnp.float32)
                updated = wet * (now + coupled[piece])
                if c == 0:
                    updated = updated + source
                rounded = updated.astype(jnp.bfloat16)
                if s + 1 < STEPS:
                    own[s + 1][h][b, piece] = rounded
                    ext[s + 1][h][b, piece] = rounded
                else:
                    final[h][b, piece] = rounded
                term = snap_b[s, b, piece] * rounded.astype(jnp.float32)
                total = term if total is None else total + term
            if s > 0:
                total = raw[h][b] + total
            raw[h][b] = total
            if s + 1 < STEPS:
                return squares
            return squares + jnp.sum((total * total).reshape(cells // 8, 8, LANES), axis=0)

        return lax.fori_loop(0, owned, one_row, jnp.zeros((8, LANES), jnp.float32), unroll=UNROLL)

    def line_copy(h, j):
        return pltpu.make_async_remote_copy(
            src_ref=mine[h],
            dst_ref=from_line[h].at[j - 1],
            send_sem=line_send.at[h, j - 1],
            recv_sem=line_recv.at[h, j - 1],
            device_id=(line_peer(j),),
            device_id_type=MESH,
        )

    def plane_copy(h, j):
        return pltpu.make_async_remote_copy(
            src_ref=line_sum[h],
            dst_ref=from_plane[h].at[j - 1],
            send_sem=plane_send.at[h, j - 1],
            recv_sem=plane_recv.at[h, j - 1],
            device_id=(plane_peer(j),),
            device_id_type=MESH,
        )

    def reduce_line_start(h, squares):
        mine[h][...] = jnp.sum(squares, axis=0, keepdims=True)
        for j in range(1, line):
            line_copy(h, j).start()

    def reduce_plane_start(h):
        total = mine[h][...]
        for j in range(1, line):
            line_copy(h, j).wait_recv()
            total = total + from_line[h][j - 1]
        line_sum[h][...] = total
        for j in range(1, planes):
            plane_copy(h, j).start()

    def finish(h):
        total = line_sum[h][...]
        for j in range(1, planes):
            plane_copy(h, j).wait_recv()
            total = total + from_plane[h][j - 1]
        meansq = total / (devices * owned * cells)
        scale = lax.rsqrt(meansq + 1e-6)
        for b in range(owned):
            sens[h][b] = raw[h][b] * scale
        copy = pltpu.make_async_copy(
            sens[h], sens_out.at[:, :, pl.ds(h * LANES, LANES)], out_sem.at[1, h]
        )
        copy.start()
        return copy

    def put_final(h):
        copy = pltpu.make_async_copy(
            final[h], adj_out.at[:, :, pl.ds(h * LANES, LANES)], out_sem.at[0, h]
        )
        copy.start()
        return copy

    for h in range(2):
        await_halo(0, h)
        if h == 0:
            send(0, 1, "held")
        advance(0, h)
        gather(1, h)
        send(1, h)

    puts = []
    await_halo(1, 0)
    squares = advance(1, 0)
    reduce_line_start(0, squares)
    puts.append(put_final(0))
    await_halo(1, 1)
    reduce_plane_start(0)
    squares = advance(1, 1)
    reduce_line_start(1, squares)
    puts.append(put_final(1))
    puts.append(finish(0))
    reduce_plane_start(1)
    puts.append(finish(1))

    for s in range(STEPS):
        for h in range(2):
            for group in range(4):

                @pl.when(exists[group])
                def _():
                    halo_copy(s, h, group).wait_send()

    for h in range(2):
        for j in range(1, line):
            line_copy(h, j).wait_send()
        for j in range(1, planes):
            plane_copy(h, j).wait_send()
    for copy in puts:
        copy.wait()


def per_device(
    adjoint_end,
    operator_blocks,
    block_cols,
    halo_send,
    wet_cells,
    gauge_cells,
    window_first,
    window_len,
    gauge_gain,
    snapshots,
):
    devices = lax.axis_size("dom")
    owned, rows, width = adjoint_end.shape
    entries = operator_blocks.shape[1]
    cells = rows // 3
    line = 8
    bf16, f32, i32 = jnp.bfloat16, jnp.float32, jnp.int32
    slots = 2 * owned + 1
    scratch = (
        [pltpu.VMEM((owned, entries, rows, rows), bf16)]
        + [pltpu.VMEM((slots, rows, LANES), bf16)] * 4
        + [pltpu.VMEM((owned, rows, LANES), bf16)] * 4
        + [pltpu.VMEM((owned, rows, LANES), bf16)] * 4
        + [pltpu.VMEM((owned, rows, LANES), bf16)] * 2
        + [pltpu.VMEM((owned, cells, LANES), f32)] * 2
        + [pltpu.VMEM((owned, cells, LANES), f32)] * 2
        + [
            pltpu.VMEM((STEPS, owned, rows, LANES), f32),
            pltpu.VMEM((owned, cells, LANES), f32),
            pltpu.VMEM((LANES, LANES), f32),
            pltpu.SMEM(block_cols.shape, i32),
            pltpu.SMEM((1, 2, 4), i32),
        ]
        + [pltpu.VMEM((1, width), i32)] * 3
        + [pltpu.VMEM((1, width), f32)]
        + [pltpu.VMEM((1, LANES), f32)] * 4
        + [pltpu.VMEM((line - 1, 1, LANES), f32)] * 2
        + [pltpu.VMEM((devices // line - 1, 1, LANES), f32)] * 2
        + [
            pltpu.SemaphoreType.DMA((17,)),
            pltpu.SemaphoreType.DMA((owned,)),
            pltpu.SemaphoreType.DMA((STEPS, 2, 4)),
            pltpu.SemaphoreType.DMA((STEPS, 2, 4)),
            pltpu.SemaphoreType.DMA((2, line - 1)),
            pltpu.SemaphoreType.DMA((2, line - 1)),
            pltpu.SemaphoreType.DMA((2, devices // line - 1)),
            pltpu.SemaphoreType.DMA((2, devices // line - 1)),
            pltpu.SemaphoreType.DMA((2, 2)),
            pltpu.VMEM(wet_cells.shape, i32),
        ]
    )
    anywhere = pl.BlockSpec(memory_space=pl.ANY)
    row = lambda v: v.reshape(1, width)
    turned_lists = jnp.swapaxes(halo_send, 1, 2)
    return pl.pallas_call(
        functools.partial(kernel, devices, line),
        out_shape=(
            jax.ShapeDtypeStruct(adjoint_end.shape, bf16),
            jax.ShapeDtypeStruct((owned, cells, width), f32),
        ),
        in_specs=[anywhere] * 10,
        out_specs=(anywhere, anywhere),
        scratch_shapes=scratch,
        compiler_params=pltpu.CompilerParams(
            collective_id=0, has_side_effects=True, vmem_limit_bytes=VM * 1024 * 1024
        ),
        name="adjoint",
    )(
        *(pltpu.with_memory_space_constraint(v, pltpu.HBM) for v in (adjoint_end, operator_blocks, block_cols, turned_lists, wet_cells, row(gauge_cells), row(window_first), row(window_len), row(gauge_gain), snapshots))
    )


def solution(mesh):
    return jax.shard_map(
        per_device,
        mesh=mesh,
        in_specs=(
            P("dom", None, None),
            P("dom", None, None, None),
            P("dom", None),
            P("dom", None, None),
            P("dom", None),
            P(),
            P(),
            P(),
            P(),
            P(None, "dom", None),
        ),
        out_specs=(P("dom", None, None), P("dom", None, None)),
        check_vma=False,
    )
```
